32 devices in a mesh: fibre: 2 (over y), chan: 8 (over z, core), tm: 2 (over x).
Axes of the slice: x: 2, y: 2, z: 4, core: 2. Of those that a mesh axis runs over, the one named last changes fastest.
Arguments:
- raw_strain: bfloat16 [2, 2560, 512], P('tm', 'fibre', 'chan'), parts along dimension 1, may hold values from -400 to 400
- fir_taps: bfloat16 [64], replicated, may hold values from -0.75 to 0.75
- live_mask: int32 [2560], P(('fibre', 'chan')), parts along dimension 0, may hold values 0 or 1
Outputs:
- correlations: bfloat16 [2560, 256, 256], P(('fibre', 'chan'), 'tm'), parts along dimension 0
The draws below stay inside these ranges and needn't reach their ends.
There are 2 independent parts, one for each index of `fibre`. The reference program is written for one: setup_inputs(seed, part) draws one part's arguments, and reference() takes and returns one part's arrays. A program takes and returns all parts, laid end to end along the dimension named above; an argument that names none is the same for every part. Nothing has to cross between parts.
All inputs are finite; a program needn't handle non-finite values. No bound on the sum of `live_mask` on one device may be relied on, other than what follows from the above.
Results may differ from the reference program's by a relative error of at most 0.0075.
Values may be sent and summed in bfloat16 or wider, within the bound.
A program may use at most 64 MiB of HBM per device.

```python
import math
import jax
import jax.numpy as jnp
from jax import lax

OFF = 256
LAG = 128
CHB = 160
TAPS = 64
STRIDE = 4
CH = 1280
NT = 128
RAW = 512
HIST = 60
WIN = 2
N_CHAN = 8


def draw_raw_strain(key, part):
    noise_key, chan_key, envelope_key = jax.random.split(jax.random.fold_in(key, 7), 3)
    noise = jnp.clip(jax.random.normal(noise_key, (WIN, CH, RAW), jnp.float32), -4.0, 4.0)
    chan_scale = jnp.exp(jax.random.uniform(chan_key, (1, CH, 1), jnp.float32, 0.0, math.log(10.0)))
    envelope = jnp.exp(jax.random.uniform(envelope_key, (WIN, CH, RAW // TAPS, 1), jnp.float32, 0.0, math.log(10.0)))
    shaped = (noise.reshape(WIN, CH, RAW // TAPS, TAPS) * envelope).reshape(WIN, CH, RAW)
    return (shaped * chan_scale).astype(jnp.bfloat16)


def set_ends(result, key, least, high):
    shape = result.shape
    place = [jax.random.randint(jax.random.fold_in(key, axis), (), 0, shape[axis]) for axis in range(len(shape))]
    result = result.at[tuple(place)].set(least)
    longest = shape.index(max(shape))
    place[longest] = (place[longest] + 1) % shape[longest]
    return result.at[tuple(place)].set(high)


def normal_values(rng, dims, scale, bound, held_as=jnp.bfloat16):
    entries = scale * jax.random.normal(rng, dims, jnp.float32)
    return jnp.clip(entries, min=-bound, max=bound).astype(held_as)


def setup_inputs(seed: int = 0, part: int = 0) -> dict:
    arg_keys = jax.random.split(jax.random.key(seed), 4)
    part_splits = jax.random.split(jax.random.fold_in(arg_keys[3], part), 4)
    raw_strain = draw_raw_strain(jax.random.fold_in(jax.random.fold_in(arg_keys[3], part), 71), part)
    fir_taps = normal_values(arg_keys[1], (TAPS,), TAPS ** -0.5, 0.75)
    live_mask = set_ends((jax.random.randint(part_splits[2], (CH,), 0, 16) < 15).astype(jnp.int32), jax.random.fold_in(part_splits[2], 1), 0, 1)
    return dict(raw_strain=raw_strain, fir_taps=fir_taps, live_mask=live_mask)


def reference(raw_strain, fir_taps, live_mask):
    raw_values = raw_strain.astype(jnp.float32)
    padded_raw = jnp.pad(raw_values, ((0, 0), (0, 0), (HIST, 0)))
    grouped = padded_raw.reshape(WIN, CH, (HIST + RAW) // STRIDE, STRIDE)
    reversed_taps = fir_taps.astype(jnp.float32)[::-1]
    filtered = jnp.zeros((WIN, CH, NT), jnp.float32)
    for block in range(TAPS // STRIDE):
        filtered = filtered + jnp.einsum('wcns,s->wcn', grouped[:, :, block:block + NT, :], reversed_taps[block * STRIDE:(block + 1) * STRIDE], precision=lax.Precision.HIGHEST)
    decimated = filtered.astype(jnp.bfloat16).astype(jnp.float32)
    loudness = jnp.sqrt(lax.optimization_barrier(jnp.mean(decimated * decimated, axis=2)) + 1e-06)
    alive_flags = live_mask.astype(jnp.float32)
    whitened = (decimated * (alive_flags[None, :, None] / loudness[:, :, None])).astype(jnp.bfloat16).astype(jnp.float32)
    lag_count = 2 * LAG
    padded_x = jnp.pad(whitened, ((0, 0), (0, 0), (lag_count, lag_count)))
    padded_y = jnp.pad(whitened, ((0, 0), (0, OFF + 1), (LAG, LAG)))
    lag_index = jnp.arange(lag_count, dtype=jnp.int32)
    row_index = jnp.arange(NT + lag_count, dtype=jnp.int32)
    toeplitz_index = row_index[None, :] - lag_index[:, None] + lag_count
    norm_scale = 1.0 / math.sqrt(NT * WIN)

    def per_group(group_index):
        first_chan = (group_index * CHB).astype(jnp.int32)
        chosen = lax.dynamic_slice_in_dim(padded_x, first_chan, CHB, 1)
        toeplitz = chosen[:, :, toeplitz_index]
        members = first_chan + 1 + jnp.arange(CHB, dtype=jnp.int32)
        partner = jax.vmap(lambda start_row: lax.dynamic_slice_in_dim(padded_y, start_row, OFF, 1))(members)
        lag_sums = jnp.einsum('gwor,wglr->glo', partner, toeplitz, precision=lax.Precision.HIGHEST)
        return (lag_sums * norm_scale).astype(jnp.bfloat16)
    stacked = lax.map(per_group, jnp.arange(N_CHAN, dtype=jnp.int32))
    return stacked.reshape(CH, lag_count, OFF)
```

```python
import functools
import math

import jax
import jax.numpy as jnp
from jax import lax
from jax.experimental import pallas as pl
from jax.experimental.pallas import tpu as pltpu
from jax.sharding import PartitionSpec as P

OFF = 256
LAG = 128
TAPS = 64
STRIDE = 4
HIST = 60
LANES = 128
SUB = 16
MESH = pl.DeviceIdType.MESH


def tap_block(taps_row, member, members, tract_len, rows):
    width = members * tract_len
    tap = lax.broadcasted_iota(jnp.int32, (TAPS, width), 0)
    lane = lax.broadcasted_iota(jnp.int32, (TAPS, width), 1)
    flip = jnp.where(tap + lane == TAPS - 1, 1.0, 0.0).astype(jnp.bfloat16)
    reversed_row = jnp.dot(
        jnp.broadcast_to(taps_row, (8, TAPS)), flip, preferred_element_type=jnp.float32
    )[0:1]
    start = (member * tract_len - HIST) % width
    rolled = pltpu.roll(
        jnp.broadcast_to(reversed_row, (rows, width)), start, 1, stride=STRIDE, stride_axis=0
    )
    row = lax.broadcasted_iota(jnp.int32, (rows, width), 0)
    local = lax.broadcasted_iota(jnp.int32, (rows, width), 1) - member * tract_len
    index = STRIDE * row + STRIDE - 1 - local
    keep = (local >= 0) & (local < tract_len) & (index >= 0) & (index < TAPS)
    return jnp.where(keep, rolled, 0.0).astype(jnp.bfloat16)


def prepare_kernel(
    n_chan,
    n_tm,
    members,
    raw_ref,
    taps_ref,
    mask_ref,
    out_ref,
    packed,
    received,
    fir,
    white,
    extended,
    send_a,
    recv_a,
    send_b,
    recv_b,
):
    me = lax.axis_index("chan")
    my_tm = lax.axis_index("tm")
    tract_len = raw_ref.shape[2]
    channels, samples = white.shape
    part = channels // members
    width = members * tract_len
    outputs = tract_len // STRIDE
    reach = -(-OFF // channels)

    barrier = pltpu.get_barrier_semaphore()
    for step in range(n_chan):
        for turn in range(n_tm):
            if step or turn:
                pl.semaphore_signal(
                    barrier,
                    inc=1,
                    device_id={
                        "chan": lax.rem(me + step, n_chan),
                        "tm": lax.rem(my_tm + turn, n_tm),
                    },
                    device_id_type=MESH,
                )
    for block in range(n_chan):
        pieces = [
            raw_ref[0, block * channels + m * part : block * channels + (m + 1) * part, :]
            for m in range(members)
        ]
        packed[block] = jnp.concatenate(pieces, axis=1)
    pl.semaphore_wait(barrier, n_chan * n_tm - 1)

    spread = []
    for step in range(1, n_chan):
        copy = pltpu.make_async_remote_copy(
            src_ref=packed.at[lax.rem(me + step, n_chan)],
            dst_ref=received.at[me],
            send_sem=send_a.at[step],
            recv_sem=recv_a.at[step],
            device_id={"chan": lax.rem(me + step, n_chan)},
            device_id_type=MESH,
        )
        copy.start()
        spread.append(copy)
    received[me] = packed[me]

    fir[...] = jnp.zeros_like(fir)
    taps_row = taps_ref[...]
    rows = 2 * outputs
    for m in range(members):
        block = tap_block(taps_row, m, members, tract_len, rows)
        for source in range(n_chan):
            first = m * samples + source * outputs
            count = min(rows, samples - source * outputs)
            fir[first : first + count, source * width : (source + 1) * width] = block[:count]
    alive = mask_ref[...].astype(jnp.float32)
    diagonal = lax.broadcasted_iota(jnp.int32, (channels, channels), 0) == lax.broadcasted_iota(
        jnp.int32, (channels, channels), 1
    )
    alive_column = jnp.sum(
        jnp.where(diagonal, jnp.broadcast_to(alive, (channels, channels)), 0.0),
        axis=1,
        keepdims=True,
    )
    for k in range(1, reach + 1):
        count = min(channels, OFF - (k - 1) * channels)

        @pl.when(me + k >= n_chan)
        def _():
            extended[k * channels : k * channels + count, :] = jnp.zeros(
                (count, extended.shape[1]), extended.dtype
            )

    for copy in spread:
        copy.wait_recv()
    tracts = jnp.concatenate([received[d] for d in range(n_chan)], axis=1)
    filtered = lax.dot_general(
        tracts, fir[...], (((1,), (1,)), ((), ())), preferred_element_type=jnp.float32
    )
    for m in range(members):
        decimated = filtered[:, m * samples : (m + 1) * samples]
        decimated = decimated.astype(jnp.bfloat16).astype(jnp.float32)
        loudness = jnp.sqrt(jnp.mean(decimated * decimated, axis=1, keepdims=True) + 1e-06)
        gain = alive_column[m * part : (m + 1) * part] / loudness
        white[m * part : (m + 1) * part, :] = (decimated * gain).astype(jnp.bfloat16)

    def share(k, turn):
        count = channels if k == 0 else min(channels, OFF - (k - 1) * channels)
        window = pl.multiple_of(my_tm * samples, LANES)
        return pltpu.make_async_remote_copy(
            src_ref=white.at[pl.ds(0, count), :],
            dst_ref=extended.at[pl.ds(k * channels, count), pl.ds(window, samples)],
            send_sem=send_b.at[k, turn],
            recv_sem=recv_b.at[k, turn],
            device_id={"chan": me - k, "tm": lax.rem(my_tm + turn, n_tm)},
            device_id_type=MESH,
        )

    pairs = [(k, t) for k in range(reach, -1, -1) for t in range(n_tm - 1, -1, -1) if k or t]
    for k, turn in pairs:

        @pl.when(me >= k)
        def _():
            share(k, turn).start()

    own = pl.multiple_of(my_tm * samples, LANES)
    extended[0:channels, pl.ds(own, samples)] = white[...]
    for copy in spread:
        copy.wait_send()
    for k, turn in pairs:

        @pl.when(me + k < n_chan)
        def _():
            share(k, turn).wait_recv()

        @pl.when(me >= k)
        def _():
            share(k, turn).wait_send()

    out_ref[...] = extended[...]


def prepare(raw_strain, fir_taps, live_mask, n_chan, n_tm):
    _, all_channels, tract_len = raw_strain.shape
    channels = all_channels // n_chan
    samples = tract_len * n_chan // STRIDE
    members = max(1, LANES // tract_len)
    part = channels // members
    width = members * tract_len
    reach = -(-OFF // channels)
    vmem = pl.BlockSpec(memory_space=pltpu.VMEM)
    return pl.pallas_call(
        functools.partial(prepare_kernel, n_chan, n_tm, members),
        out_shape=jax.ShapeDtypeStruct((channels + OFF, n_tm * samples), jnp.bfloat16),
        in_specs=[vmem, vmem, vmem],
        out_specs=vmem,
        scratch_shapes=[
            pltpu.VMEM((n_chan, part, width), jnp.bfloat16),
            pltpu.VMEM((n_chan, part, width), jnp.bfloat16),
            pltpu.VMEM((members * samples, n_chan * width), jnp.bfloat16),
            pltpu.VMEM((channels, samples), jnp.bfloat16),
            pltpu.VMEM((channels + OFF, n_tm * samples), jnp.bfloat16),
            pltpu.SemaphoreType.DMA((n_chan,)),
            pltpu.SemaphoreType.DMA((n_chan,)),
            pltpu.SemaphoreType.DMA((reach + 1, n_tm)),
            pltpu.SemaphoreType.DMA((reach + 1, n_tm)),
        ],
        compiler_params=pltpu.CompilerParams(collective_id=0, has_side_effects=True),
        name="prepare",
    )(raw_strain, fir_taps.reshape(1, TAPS), live_mask.reshape(1, channels))


def correlate_kernel(windows, samples, lag_dev, ext_ref, out_ref, wide, shifted):
    phase = pl.program_id(0)
    groups = out_ref.shape[0]
    rows = ext_ref.shape[0]
    first_lag = lax.axis_index("tm") * lag_dev - LAG
    norm_scale = 1.0 / math.sqrt(samples * windows)

    @pl.when(phase == 0)
    def _():
        wide[0:rows, :] = ext_ref[...].astype(jnp.float32)
        wide[rows : rows + 8, :] = jnp.zeros((8, wide.shape[1]), jnp.float32)

    chosen = [wide[g * SUB : g * SUB + 1, :] for g in range(groups)]
    moved = wide[1 : rows + 1, :]
    shifted[...] = moved[: shifted.shape[0]].astype(jnp.bfloat16)
    wide[0:rows, :] = moved
    lag = first_lag + lax.broadcasted_iota(jnp.int32, (lag_dev, samples), 0)
    at = lax.broadcasted_iota(jnp.int32, (lag_dev, samples), 1) - lag
    keep = (at >= 0) & (at < samples)
    if lag_dev % samples == 0 and LAG % samples == 0:
        turn = None
    else:
        turn = lax.rem(first_lag + samples * (-(-LAG // samples)), samples)
    for g in range(groups):
        row = chosen[g]
        parts = []
        for w in range(windows):
            trace = row[:, w * samples : (w + 1) * samples]
            if turn is not None:
                trace = pltpu.roll(jnp.broadcast_to(trace, (8, samples)), turn, 1)[0:1]
            trace = jnp.broadcast_to(trace, (lag_dev, samples))
            rolled = pltpu.roll(trace, 0, 1, stride=1, stride_axis=0)
            parts.append(jnp.where(keep, rolled, 0.0).astype(jnp.bfloat16))
        toeplitz = jnp.concatenate(parts, axis=1)
        sums = lax.dot_general(
            toeplitz,
            shifted[g * SUB : g * SUB + OFF, :],
            (((1,), (1,)), ((), ())),
            preferred_element_type=jnp.float32,
        )
        out_ref[g, 0] = (sums * norm_scale).astype(jnp.bfloat16)


def correlate(extended, channels, windows, lag_dev):
    depth = extended.shape[1]
    samples = depth // windows
    groups = channels // SUB
    out = pl.pallas_call(
        functools.partial(correlate_kernel, windows, samples, lag_dev),
        out_shape=jax.ShapeDtypeStruct((groups, SUB, lag_dev, OFF), jnp.bfloat16),
        grid=(SUB,),
        in_specs=[pl.BlockSpec(extended.shape, lambda r: (0, 0))],
        out_specs=pl.BlockSpec((groups, 1, lag_dev, OFF), lambda r: (0, r, 0, 0)),
        scratch_shapes=[
            pltpu.VMEM((extended.shape[0] + 8, depth), jnp.float32),
            pltpu.VMEM(((groups - 1) * SUB + OFF, depth), jnp.bfloat16),
        ],
        name="correlate",
    )(extended)
    return out.reshape(channels, lag_dev, OFF)


def shards(raw_strain, fir_taps, live_mask):
    n_chan = lax.axis_size("chan")
    n_tm = lax.axis_size("tm")
    extended = prepare(raw_strain, fir_taps, live_mask, n_chan, n_tm)
    return correlate(extended, live_mask.shape[0], n_tm, 2 * LAG // n_tm)


def solution(mesh):
    placed = (P("tm", "fibre", "chan"), P(), P(("fibre", "chan")))
    return jax.shard_map(
        shards,
        mesh=mesh,
        in_specs=placed,
        out_specs=P(("fibre", "chan"), "tm", None),
        check_vma=False,
    )
```

```python
import functools
import math

import jax
import jax.numpy as jnp
from jax import lax
from jax.experimental import pallas as pl
from jax.experimental.pallas import tpu as pltpu
from jax.sharding import PartitionSpec as P

OFF = 256
LAG = 128
TAPS = 64
STRIDE = 4
HIST = 60
LANES = 128
SUB = 16
MESH = pl.DeviceIdType.MESH


def tap_block(taps_row, member, members, tract_len, rows):
    width = members * tract_len
    tap = lax.broadcasted_iota(jnp.int32, (TAPS, width), 0)
    lane = lax.broadcasted_iota(jnp.int32, (TAPS, width), 1)
    flip = jnp.where(tap + lane == TAPS - 1, 1.0, 0.0).astype(jnp.bfloat16)
    reversed_row = jnp.dot(
        jnp.broadcast_to(taps_row, (8, TAPS)), flip, preferred_element_type=jnp.float32
    )[0:1]
    start = (member * tract_len - HIST) % width
    rolled = pltpu.roll(
        jnp.broadcast_to(reversed_row, (rows, width)), start, 1, stride=STRIDE, stride_axis=0
    )
    row = lax.broadcasted_iota(jnp.int32, (rows, width), 0)
    local = lax.broadcasted_iota(jnp.int32, (rows, width), 1) - member * tract_len
    index = STRIDE * row + STRIDE - 1 - local
    keep = (local >= 0) & (local < tract_len) & (index >= 0) & (index < TAPS)
    return jnp.where(keep, rolled, 0.0).astype(jnp.bfloat16)


def prepare_kernel(
    n_chan,
    n_tm,
    members,
    raw_ref,
    taps_ref,
    mask_ref,
    out_ref,
    packed,
    received,
    fir,
    white,
    extended,
    send_a,
    recv_a,
    send_b,
    recv_b,
):
    me = lax.axis_index("chan")
    my_tm = lax.axis_index("tm")
    tract_len = raw_ref.shape[1]
    channels, samples = white.shape
    part = channels // members
    width = members * tract_len
    outputs = tract_len // STRIDE
    reach = -(-OFF // channels)

    barrier = pltpu.get_barrier_semaphore()
    for step in range(n_chan):
        for turn in range(n_tm):
            if step or turn:
                pl.semaphore_signal(
                    barrier,
                    inc=1,
                    device_id={
                        "chan": lax.rem(me + step, n_chan),
                        "tm": lax.rem(my_tm + turn, n_tm),
                    },
                    device_id_type=MESH,
                )
    turned = raw_ref[0].astype(jnp.float32).T.astype(jnp.bfloat16)
    for block in range(n_chan):
        first = block * channels
        pieces = [turned[first + m * part : first + (m + 1) * part] for m in range(members)]
        packed[block] = jnp.concatenate(pieces, axis=1)
    pl.semaphore_wait(barrier, n_chan * n_tm - 1)

    spread = []
    for step in range(1, n_chan):
        copy = pltpu.make_async_remote_copy(
            src_ref=packed.at[lax.rem(me + step, n_chan)],
            dst_ref=received.at[me],
            send_sem=send_a.at[step],
            recv_sem=recv_a.at[step],
            device_id={"chan": lax.rem(me + step, n_chan)},
            device_id_type=MESH,
        )
        copy.start()
        spread.append(copy)
    received[me] = packed[me]

    fir[...] = jnp.zeros_like(fir)
    taps_row = taps_ref[...]
    rows = 2 * outputs
    for m in range(members):
        block = tap_block(taps_row, m, members, tract_len, rows)
        for source in range(n_chan):
            first = m * samples + source * outputs
            count = min(rows, samples - source * outputs)
            fir[first : first + count, source * width : (source + 1) * width] = block[:count]
    alive = mask_ref[...].astype(jnp.float32)
    diagonal = lax.broadcasted_iota(jnp.int32, (channels, channels), 0) == lax.broadcasted_iota(
        jnp.int32, (channels, channels), 1
    )
    alive_column = jnp.sum(
        jnp.where(diagonal, jnp.broadcast_to(alive, (channels, channels)), 0.0),
        axis=1,
        keepdims=True,
    )
    for k in range(1, reach + 1):
        count = min(channels, OFF - (k - 1) * channels)

        @pl.when(me + k >= n_chan)
        def _():
            extended[k * channels : k * channels + count, :] = jnp.zeros(
                (count, extended.shape[1]), extended.dtype
            )

    for copy in spread:
        copy.wait_recv()
    tracts = jnp.concatenate([received[d] for d in range(n_chan)], axis=1)
    filtered = lax.dot_general(
        tracts, fir[...], (((1,), (1,)), ((), ())), preferred_element_type=jnp.float32
    )
    for m in range(members):
        decimated = filtered[:, m * samples : (m + 1) * samples]
        decimated = decimated.astype(jnp.bfloat16).astype(jnp.float32)
        loudness = jnp.sqrt(jnp.mean(decimated * decimated, axis=1, keepdims=True) + 1e-06)
        gain = alive_column[m * part : (m + 1) * part] / loudness
        white[m * part : (m + 1) * part, :] = (decimated * gain).astype(jnp.bfloat16)

    def share(k, turn):
        count = channels if k == 0 else min(channels, OFF - (k - 1) * channels)
        window = pl.multiple_of(my_tm * samples, LANES)
        return pltpu.make_async_remote_copy(
            src_ref=white.at[pl.ds(0, count), :],
            dst_ref=extended.at[pl.ds(k * channels, count), pl.ds(window, samples)],
            send_sem=send_b.at[k, turn],
            recv_sem=recv_b.at[k, turn],
            device_id={"chan": me - k, "tm": lax.rem(my_tm + turn, n_tm)},
            device_id_type=MESH,
        )

    pairs = [(k, t) for k in range(reach, -1, -1) for t in range(n_tm - 1, -1, -1) if k or t]
    for k, turn in pairs:

        @pl.when(me >= k)
        def _():
            share(k, turn).start()

    own = pl.multiple_of(my_tm * samples, LANES)
    extended[0:channels, pl.ds(own, samples)] = white[...]
    for copy in spread:
        copy.wait_send()
    for k, turn in pairs:

        @pl.when(me + k < n_chan)
        def _():
            share(k, turn).wait_recv()

        @pl.when(me >= k)
        def _():
            share(k, turn).wait_send()

    out_ref[...] = extended[...]


def prepare(raw_strain, fir_taps, live_mask, n_chan, n_tm):
    _, all_channels, tract_len = raw_strain.shape
    channels = all_channels // n_chan
    samples = tract_len * n_chan // STRIDE
    members = max(1, LANES // tract_len)
    part = channels // members
    width = members * tract_len
    reach = -(-OFF // channels)
    vmem = pl.BlockSpec(memory_space=pltpu.VMEM)
    return pl.pallas_call(
        functools.partial(prepare_kernel, n_chan, n_tm, members),
        out_shape=jax.ShapeDtypeStruct((channels + OFF, n_tm * samples), jnp.bfloat16),
        in_specs=[vmem, vmem, vmem],
        out_specs=vmem,
        scratch_shapes=[
            pltpu.VMEM((n_chan, part, width), jnp.bfloat16),
            pltpu.VMEM((n_chan, part, width), jnp.bfloat16),
            pltpu.VMEM((members * samples, n_chan * width), jnp.bfloat16),
            pltpu.VMEM((channels, samples), jnp.bfloat16),
            pltpu.VMEM((channels + OFF, n_tm * samples), jnp.bfloat16),
            pltpu.SemaphoreType.DMA((n_chan,)),
            pltpu.SemaphoreType.DMA((n_chan,)),
            pltpu.SemaphoreType.DMA((reach + 1, n_tm)),
            pltpu.SemaphoreType.DMA((reach + 1, n_tm)),
        ],
        compiler_params=pltpu.CompilerParams(collective_id=0, has_side_effects=True),
        name="prepare",
    )(raw_strain.transpose(0, 2, 1), fir_taps.reshape(1, TAPS), live_mask.reshape(1, channels))


def correlate_kernel(windows, samples, lag_dev, ext_ref, out_ref, wide):
    group = pl.program_id(0)
    first_lag = lax.axis_index("tm") * lag_dev - LAG
    norm_scale = 1.0 / math.sqrt(samples * windows)
    rows = ext_ref.shape[0]

    @pl.when(group == 0)
    def _():
        wide[0:rows, :] = ext_ref[...]
        wide[rows:, :] = jnp.zeros((wide.shape[0] - rows, wide.shape[1]), wide.dtype)

    base = pl.multiple_of(group * SUB, SUB)
    own = wide[pl.ds(base, SUB), :].astype(jnp.float32)
    partners = wide[pl.ds(base, OFF), :]
    beyond = wide[pl.ds(pl.multiple_of(base + OFF, SUB), LANES), :]
    lag = first_lag + lax.broadcasted_iota(jnp.int32, (lag_dev, samples), 0)
    at = lax.broadcasted_iota(jnp.int32, (lag_dev, samples), 1) - lag
    keep = (at >= 0) & (at < samples)
    lane = lax.broadcasted_iota(jnp.int32, (lag_dev, LANES), 1)
    if lag_dev % samples == 0 and LAG % samples == 0:
        turn = None
    else:
        turn = lax.rem(first_lag + samples * (-(-LAG // samples)), samples)
    blocks = []
    for r in range(SUB):
        parts = []
        for w in range(windows):
            trace = own[r : r + 1, w * samples : (w + 1) * samples]
            if turn is not None:
                trace = pltpu.roll(jnp.broadcast_to(trace, (8, samples)), turn, 1)[0:1]
            trace = jnp.broadcast_to(trace, (lag_dev, samples))
            rolled = pltpu.roll(trace, 0, 1, stride=1, stride_axis=0)
            parts.append(jnp.where(keep, rolled, 0.0).astype(jnp.bfloat16))
        blocks.append(jnp.concatenate(parts, axis=1))
    toeplitz = jnp.concatenate(blocks, axis=0)
    contract = (((1,), (1,)), ((), ()))
    near = lax.dot_general(toeplitz, partners, contract, preferred_element_type=jnp.float32)
    far = lax.dot_general(toeplitz, beyond, contract, preferred_element_type=jnp.float32)
    for r in range(SUB):
        first = r * lag_dev
        skip = r + 1
        columns = [
            near[first : first + lag_dev, k * LANES : (k + 1) * LANES] for k in range(OFF // LANES)
        ]
        columns[0] = jnp.where(lane < skip, far[first : first + lag_dev], columns[0])
        columns = [(c * norm_scale).astype(jnp.bfloat16).astype(jnp.float32) for c in columns]
        turned = [pltpu.roll(column, LANES - skip, 1) for column in columns]
        for k in range(len(columns)):
            following = turned[(k + 1) % len(columns)]
            value = jnp.where(lane < LANES - skip, turned[k], following)
            out_ref[r, :, k * LANES : (k + 1) * LANES] = value.astype(jnp.bfloat16)


def correlate(extended, channels, windows, lag_dev):
    depth = extended.shape[1]
    samples = depth // windows
    return pl.pallas_call(
        functools.partial(correlate_kernel, windows, samples, lag_dev),
        out_shape=jax.ShapeDtypeStruct((channels, lag_dev, OFF), jnp.bfloat16),
        grid=(channels // SUB,),
        in_specs=[pl.BlockSpec(extended.shape, lambda g: (0, 0))],
        out_specs=pl.BlockSpec((SUB, lag_dev, OFF), lambda g: (g, 0, 0)),
        scratch_shapes=[pltpu.VMEM((channels - SUB + OFF + LANES, depth), jnp.bfloat16)],
        name="correlate",
    )(extended)


def shards(raw_strain, fir_taps, live_mask):
    n_chan = lax.axis_size("chan")
    n_tm = lax.axis_size("tm")
    extended = prepare(raw_strain, fir_taps, live_mask, n_chan, n_tm)
    return correlate(extended, live_mask.shape[0], n_tm, 2 * LAG // n_tm)


def solution(mesh):
    placed = (P("tm", "fibre", "chan"), P(), P(("fibre", "chan")))
    return jax.shard_map(
        shards,
        mesh=mesh,
        in_specs=placed,
        out_specs=P(("fibre", "chan"), "tm", None),
        check_vma=False,
    )
```

```python
import functools
import math

import jax
import jax.numpy as jnp
from jax import lax
from jax.experimental import pallas as pl
from jax.experimental.pallas import tpu as pltpu
from jax.sharding import PartitionSpec as P

OFF = 256
LAG = 128
TAPS = 64
STRIDE = 4
HIST = 60
LANES = 128
SUB = 16
VMEM_GRANT = 28 * 2**20
MESH = pl.DeviceIdType.MESH


def tap_block(taps_row, member, members, tract_len, rows):
    width = members * tract_len
    tap = lax.broadcasted_iota(jnp.int32, (TAPS, width), 0)
    lane = lax.broadcasted_iota(jnp.int32, (TAPS, width), 1)
    flip = jnp.where(tap + lane == TAPS - 1, 1.0, 0.0).astype(jnp.bfloat16)
    reversed_row = jnp.dot(
        jnp.broadcast_to(taps_row, (8, TAPS)), flip, preferred_element_type=jnp.float32
    )[0:1]
    start = (member * tract_len - HIST) % width
    rolled = pltpu.roll(
        jnp.broadcast_to(reversed_row, (rows, width)), start, 1, stride=STRIDE, stride_axis=0
    )
    row = lax.broadcasted_iota(jnp.int32, (rows, width), 0)
    local = lax.broadcasted_iota(jnp.int32, (rows, width), 1) - member * tract_len
    index = STRIDE * row + STRIDE - 1 - local
    keep = (local >= 0) & (local < tract_len) & (index >= 0) & (index < TAPS)
    return jnp.where(keep, rolled, 0.0).astype(jnp.bfloat16)


def prepare_kernel(
    n_chan,
    n_tm,
    members,
    raw_ref,
    taps_ref,
    mask_ref,
    out_ref,
    packed,
    received,
    fir,
    white,
    extended,
    send_a,
    recv_a,
    send_b,
    recv_b,
):
    me = lax.axis_index("chan")
    my_tm = lax.axis_index("tm")
    tract_len = raw_ref.shape[1]
    channels, samples = white.shape
    part = channels // members
    width = members * tract_len
    outputs = tract_len // STRIDE
    reach = -(-OFF // channels)

    def signal(chan, turn):
        pl.semaphore_signal(
            barrier,
            inc=1,
            device_id={"chan": chan, "tm": lax.rem(my_tm + turn, n_tm)},
            device_id_type=MESH,
        )

    barrier = pltpu.get_barrier_semaphore()
    for step in range(1, n_chan):
        signal(lax.rem(me + step, n_chan), 0)
    for turn in range(1, n_tm):
        signal(me, turn)
        for k in range(1, reach + 1):

            @pl.when(me >= k)
            def _():
                signal(me - k, turn)

            @pl.when(me + k < n_chan)
            def _():
                signal(me + k, turn)

    turned = raw_ref[0].astype(jnp.float32).T.astype(jnp.bfloat16)
    for block in range(n_chan):
        first = block * channels
        pieces = [turned[first + m * part : first + (m + 1) * part] for m in range(members)]
        packed[block] = jnp.concatenate(pieces, axis=1)
    near_blocks = 1
    for k in range(1, reach + 1):
        near_blocks = near_blocks + (me + n_chan - k) // n_chan + 1 - (me + k) // n_chan
    pl.semaphore_wait(barrier, n_chan - 1 + (n_tm - 1) * near_blocks)

    def spread(target, slot):
        return pltpu.make_async_remote_copy(
            src_ref=packed.at[target],
            dst_ref=received.at[me],
            send_sem=send_a.at[slot],
            recv_sem=recv_a.at[me],
            device_id={"chan": target},
            device_id_type=MESH,
        )

    ways = [(distance, side) for distance in range(n_chan - 1, 0, -1) for side in range(2)]
    for distance, side in ways:
        target = me + distance if side else me - distance

        @pl.when(target < n_chan if side else target >= 0)
        def _():
            spread(target, 2 * distance + side).start()

    received[me] = packed[me]

    fir[...] = jnp.zeros_like(fir)
    taps_row = taps_ref[...]
    rows = 2 * outputs
    for m in range(members):
        block = tap_block(taps_row, m, members, tract_len, rows)
        for source in range(n_chan):
            first = m * samples + source * outputs
            count = min(rows, samples - source * outputs)
            fir[first : first + count, source * width : (source + 1) * width] = block[:count]
    alive = mask_ref[...].astype(jnp.float32)
    diagonal = lax.broadcasted_iota(jnp.int32, (channels, channels), 0) == lax.broadcasted_iota(
        jnp.int32, (channels, channels), 1
    )
    alive_column = jnp.sum(
        jnp.where(diagonal, jnp.broadcast_to(alive, (channels, channels)), 0.0),
        axis=1,
        keepdims=True,
    )
    for k in range(1, reach + 1):
        count = min(channels, OFF - (k - 1) * channels)

        @pl.when(me + k >= n_chan)
        def _():
            extended[k * channels : k * channels + count, :] = jnp.zeros(
                (count, extended.shape[1]), extended.dtype
            )

    for source in range(n_chan):

        @pl.when(me != source)
        def _():
            pltpu.make_async_remote_copy(
                src_ref=packed.at[source],
                dst_ref=received.at[source],
                send_sem=send_a.at[0],
                recv_sem=recv_a.at[source],
                device_id={"chan": source},
                device_id_type=MESH,
            ).wait_recv()

    tracts = jnp.concatenate([received[d] for d in range(n_chan)], axis=1)
    filtered = lax.dot_general(
        tracts, fir[...], (((1,), (1,)), ((), ())), preferred_element_type=jnp.float32
    )
    for m in range(members):
        decimated = filtered[:, m * samples : (m + 1) * samples]
        decimated = decimated.astype(jnp.bfloat16).astype(jnp.float32)
        loudness = jnp.sqrt(jnp.mean(decimated * decimated, axis=1, keepdims=True) + 1e-06)
        gain = alive_column[m * part : (m + 1) * part] / loudness
        white[m * part : (m + 1) * part, :] = (decimated * gain).astype(jnp.bfloat16)

    def share(k, turn):
        count = channels if k == 0 else min(channels, OFF - (k - 1) * channels)
        window = pl.multiple_of(my_tm * samples, LANES)
        return pltpu.make_async_remote_copy(
            src_ref=white.at[pl.ds(0, count), :],
            dst_ref=extended.at[pl.ds(k * channels, count), pl.ds(window, samples)],
            send_sem=send_b.at[k, turn],
            recv_sem=recv_b.at[k, turn],
            device_id={"chan": me - k, "tm": lax.rem(my_tm + turn, n_tm)},
            device_id_type=MESH,
        )

    pairs = [(k, t) for k in range(reach, -1, -1) for t in range(n_tm - 1, -1, -1) if k or t]
    for k, turn in pairs:

        @pl.when(me >= k)
        def _():
            share(k, turn).start()

    own = pl.multiple_of(my_tm * samples, LANES)
    extended[0:channels, pl.ds(own, samples)] = white[...]
    for distance, side in ways:
        target = me + distance if side else me - distance

        @pl.when(target < n_chan if side else target >= 0)
        def _():
            spread(target, 2 * distance + side).wait_send()

    for k, turn in pairs:

        @pl.when(me + k < n_chan)
        def _():
            share(k, turn).wait_recv()

        @pl.when(me >= k)
        def _():
            share(k, turn).wait_send()

    out_ref[...] = extended[...]


def prepare(raw_strain, fir_taps, live_mask, n_chan, n_tm):
    _, all_channels, tract_len = raw_strain.shape
    channels = all_channels // n_chan
    samples = tract_len * n_chan // STRIDE
    members = max(1, LANES // tract_len)
    part = channels // members
    width = members * tract_len
    reach = -(-OFF // channels)
    vmem = pl.BlockSpec(memory_space=pltpu.VMEM)
    return pl.pallas_call(
        functools.partial(prepare_kernel, n_chan, n_tm, members),
        out_shape=jax.ShapeDtypeStruct((channels + OFF, n_tm * samples), jnp.bfloat16),
        in_specs=[vmem, vmem, vmem],
        out_specs=vmem,
        scratch_shapes=[
            pltpu.VMEM((n_chan, part, width), jnp.bfloat16),
            pltpu.VMEM((n_chan, part, width), jnp.bfloat16),
            pltpu.VMEM((members * samples, n_chan * width), jnp.bfloat16),
            pltpu.VMEM((channels, samples), jnp.bfloat16),
            pltpu.VMEM((channels + OFF, n_tm * samples), jnp.bfloat16),
            pltpu.SemaphoreType.DMA((2 * n_chan,)),
            pltpu.SemaphoreType.DMA((n_chan,)),
            pltpu.SemaphoreType.DMA((reach + 1, n_tm)),
            pltpu.SemaphoreType.DMA((reach + 1, n_tm)),
        ],
        compiler_params=pltpu.CompilerParams(
            collective_id=0, has_side_effects=True, vmem_limit_bytes=VMEM_GRANT
        ),
        name="prepare",
    )(raw_strain.transpose(0, 2, 1), fir_taps.reshape(1, TAPS), live_mask.reshape(1, channels))


def correlate_kernel(windows, samples, lag_dev, ext_ref, out_ref, wide):
    group = pl.program_id(0)
    first_lag = lax.axis_index("tm") * lag_dev - LAG
    norm_scale = 1.0 / math.sqrt(samples * windows)
    rows = ext_ref.shape[0]

    @pl.when(group == 0)
    def _():
        wide[0:rows, :] = ext_ref[...]
        wide[rows:, :] = jnp.zeros((wide.shape[0] - rows, wide.shape[1]), wide.dtype)

    base = pl.multiple_of(group * SUB, SUB)
    own = wide[pl.ds(base, SUB), :].astype(jnp.float32)
    partners = wide[pl.ds(base, OFF), :]
    beyond = wide[pl.ds(pl.multiple_of(base + OFF, SUB), LANES), :]
    lag = first_lag + lax.broadcasted_iota(jnp.int32, (lag_dev, samples), 0)
    at = lax.broadcasted_iota(jnp.int32, (lag_dev, samples), 1) - lag
    keep = (at >= 0) & (at < samples)
    lane = lax.broadcasted_iota(jnp.int32, (lag_dev, LANES), 1)
    if lag_dev % samples == 0 and LAG % samples == 0:
        turn = None
    else:
        turn = lax.rem(first_lag + samples * (-(-LAG // samples)), samples)
    blocks = []
    for r in range(SUB):
        parts = []
        for w in range(windows):
            trace = own[r : r + 1, w * samples : (w + 1) * samples]
            if turn is not None:
                trace = pltpu.roll(jnp.broadcast_to(trace, (8, samples)), turn, 1)[0:1]
            trace = jnp.broadcast_to(trace, (lag_dev, samples))
            rolled = pltpu.roll(trace, 0, 1, stride=1, stride_axis=0)
            parts.append(jnp.where(keep, rolled, 0.0).astype(jnp.bfloat16))
        blocks.append(jnp.concatenate(parts, axis=1))
    toeplitz = jnp.concatenate(blocks, axis=0)
    contract = (((1,), (1,)), ((), ()))
    near = lax.dot_general(toeplitz, partners, contract, preferred_element_type=jnp.float32)
    far = lax.dot_general(toeplitz, beyond, contract, preferred_element_type=jnp.float32)
    for r in range(SUB):
        first = r * lag_dev
        skip = r + 1
        columns = [
            near[first : first + lag_dev, k * LANES : (k + 1) * LANES] for k in range(OFF // LANES)
        ]
        columns[0] = jnp.where(lane < skip, far[first : first + lag_dev], columns[0])
        columns = [(c * norm_scale).astype(jnp.bfloat16).astype(jnp.float32) for c in columns]
        turned = [pltpu.roll(column, LANES - skip, 1) for column in columns]
        for k in range(len(columns)):
            following = turned[(k + 1) % len(columns)]
            value = jnp.where(lane < LANES - skip, turned[k], following)
            out_ref[r, :, k * LANES : (k + 1) * LANES] = value.astype(jnp.bfloat16)


def correlate(extended, channels, windows, lag_dev):
    depth = extended.shape[1]
    samples = depth // windows
    return pl.pallas_call(
        functools.partial(correlate_kernel, windows, samples, lag_dev),
        out_shape=jax.ShapeDtypeStruct((channels, lag_dev, OFF), jnp.bfloat16),
        grid=(channels // SUB,),
        in_specs=[pl.BlockSpec(extended.shape, lambda g: (0, 0))],
        out_specs=pl.BlockSpec((SUB, lag_dev, OFF), lambda g: (g, 0, 0)),
        scratch_shapes=[pltpu.VMEM((channels - SUB + OFF + LANES, depth), jnp.bfloat16)],
        compiler_params=pltpu.CompilerParams(vmem_limit_bytes=VMEM_GRANT),
        name="correlate",
    )(extended)


def shards(raw_strain, fir_taps, live_mask):
    n_chan = lax.axis_size("chan")
    n_tm = lax.axis_size("tm")
    extended = prepare(raw_strain, fir_taps, live_mask, n_chan, n_tm)
    return correlate(extended, live_mask.shape[0], n_tm, 2 * LAG // n_tm)


def solution(mesh):
    placed = (P("tm", "fibre", "chan"), P(), P(("fibre", "chan")))
    return jax.shard_map(
        shards,
        mesh=mesh,
        in_specs=placed,
        out_specs=P(("fibre", "chan"), "tm", None),
        check_vma=False,
    )
```
